32 devices in a mesh: rows: 4 (over y, x), cols: 8 (over z, core).
Axes of the slice: x: 2, y: 2, z: 4, core: 2. Of those that a mesh axis runs over, the one named last changes fastest.
Arguments:
- spectra: bfloat16 [1024, 4096], P(('rows', 'cols')), may hold values from -6 to 6
- band_weights: float32 [2048], replicated, may hold values from 0.3 to 3
- lag_weights: float32 [4], replicated, may hold values from 0.5 to 2
- selected_bins: int32 [8], replicated, may hold values from 0 to 7
Outputs:
- correlations: float32 [4, 1024, 1024], P(None, 'rows', 'cols')
- gradient: float32 [1024, 4096], P(('rows', 'cols'))
The draws below stay inside these ranges and needn't reach their ends.
All inputs are finite; a program needn't handle non-finite values.
Results may differ from the reference program's by a relative error of at most 0.0045.
Values may be sent and summed in bfloat16 or wider, within the bound.
No kernel may reach another device: no remote copies, remote signals or barrier semaphores. Data moves between devices by JAX's collectives and lax.ppermute only.
A program may use at most 128 MiB of HBM per device.

```python
import math
import jax
import jax.numpy as jnp
from jax import lax

F = 2048
LAGS = 4
LAG_STEP = 8
BIN = 128
NSEL = 8
C = 1024
NBIN = 8


def place_ends(array, key, smallest, high):
    longest = array.shape.index(max(array.shape))
    spots = []
    for shift in (0, 1):
        where = [jax.random.randint(jax.random.fold_in(key, axis), (), 0, length) for axis, length in enumerate(array.shape)]
        where[longest] = (where[longest] + shift) % array.shape[longest]
        spots.append(tuple(where))
    return array.at[spots[0]].set(smallest).at[spots[1]].set(high)


def steps_of(own_key, shape, cuts, least, top_value):
    factor_of = 1.0
    for dim, parts in cuts:
        steps = jax.random.uniform(jax.random.fold_in(jax.random.fold_in(own_key, 6), dim), (parts,), jnp.float32, least / len(cuts), top_value / len(cuts))
        factor_of = factor_of * jnp.repeat(jnp.exp(steps), shape[dim] // parts).reshape((-1,) + (1,) * (len(shape) - 1 - dim))
    return factor_of


def noise(key, shape, scale, bound, pieces=(), held_as=jnp.bfloat16):
    values = jax.random.normal(key, shape, jnp.float32) * scale
    if len(pieces) > 0:
        values = steps_of(key, shape, pieces, -0.22, 0.18) * values
    return jnp.clip(values, min=-bound, max=bound).astype(held_as)


def setup_inputs(seed: int = 0) -> dict:
    keys = jax.random.split(jax.random.key(seed), 5)
    return {
        "spectra": noise(keys[0], (C, 2 * F), 1.0, 6.0, ((0, 32),)),
        "band_weights": jnp.clip(jnp.exp(jax.random.uniform(keys[1], (F,), jnp.float32, math.log(0.3), math.log(3.0))), 0.3, 3.0),
        "lag_weights": jnp.clip(jnp.exp(jax.random.uniform(keys[2], (LAGS,), jnp.float32, math.log(0.5), math.log(2.0))), 0.5, 2.0),
        "selected_bins": place_ends(jax.random.randint(keys[3], (NSEL,), 0, NBIN), jax.random.fold_in(keys[3], 1), 0, NBIN - 1).astype(jnp.int32),
    }


def reference(spectra, band_weights, lag_weights, selected_bins):
    raw = spectra.astype(jnp.float32)
    mean_power = lax.optimization_barrier(jnp.mean(raw * raw, axis=1, keepdims=True))
    bin_gains = jnp.concatenate([band_weights, band_weights])
    whitened = (raw * lax.rsqrt(mean_power + 1e-05) * bin_gains[None, :]).astype(jnp.bfloat16)
    channel = jnp.arange(C, dtype=jnp.int32)
    distance = jnp.abs(channel[:, None] - channel[None, :]) // BIN
    chosen = jnp.zeros((C, C), dtype=bool)
    for entry in range(NSEL):
        chosen = jnp.logical_or(chosen, distance == selected_bins[entry])
    selected = chosen.astype(jnp.float32)
    norm_scale = 1.0 / jnp.sqrt(jnp.float32(2 * F))
    bin_index = jnp.arange(F, dtype=jnp.float32)
    real_part = whitened[:, :F].astype(jnp.float32)
    imag_part = whitened[:, F:].astype(jnp.float32)
    outputs = []
    gradient = jnp.zeros((C, 2 * F), jnp.float32)
    for lag_index in range(LAGS):
        shift_lag = float((lag_index - LAGS // 2) * LAG_STEP)
        theta = jnp.pi * bin_index * shift_lag / F
        cosine = jnp.cos(theta)
        sine_part = jnp.sin(theta)
        rotated = jnp.concatenate([real_part * cosine - imag_part * sine_part, imag_part * cosine + real_part * sine_part], axis=1).astype(jnp.bfloat16)
        correlation = jnp.dot(rotated, whitened.T, preferred_element_type=jnp.float32) * norm_scale
        outputs.append(correlation)
        adjoint = (lag_weights[lag_index] * selected * correlation).astype(jnp.bfloat16)
        back = jnp.dot(adjoint, whitened, preferred_element_type=jnp.float32) * norm_scale
        back_real = back[:, :F]
        back_imag = back[:, F:]
        gradient = gradient + jnp.concatenate([back_real * cosine + back_imag * sine_part, back_imag * cosine - back_real * sine_part], axis=1)
        gradient = gradient + jnp.dot(adjoint.T, rotated, preferred_element_type=jnp.float32) * norm_scale
    return (jnp.stack(outputs), gradient)
```

```python
import functools
import numpy as np
import jax
import jax.numpy as jnp
from jax import lax
from jax.experimental import pallas as pl
from jax.experimental.pallas import tpu as pltpu
from jax.sharding import PartitionSpec as P

LAGS = 4
LAG_STEP = 8
BIN = 128
PAIR = 2
CHUNK = 512

LAG_SHIFTS = [(lag - LAGS // 2) * LAG_STEP for lag in range(LAGS)]
SHIFTS = sorted({s for t in LAG_SHIFTS for s in (t, -t)})
TABLE = sorted({abs(s) for s in SHIFTS if s != 0})

NT = (((1,), (1,)), ((), ()))


def phase_table(freqs):
    index = np.arange(freqs, dtype=np.float64)
    rows = []
    for shift in TABLE:
        theta = np.pi * index * shift / freqs
        rows += [np.cos(theta), np.sin(theta)]
    return jnp.asarray(np.stack(rows), jnp.float32)


def phase(table_ref, shift, cols):
    at = TABLE.index(abs(shift))
    cosine = table_ref[2 * at : 2 * at + 1, cols]
    sine = table_ref[2 * at + 1 : 2 * at + 2, cols]
    return cosine, (sine if shift > 0 else -sine)


def reverse_bits(value, n_bits):
    return sum(((value >> b) & 1) << (n_bits - 1 - b) for b in range(n_bits))


def whiten_kernel(raw_ref, gain_ref, out_ref):
    freqs = gain_ref.shape[1]
    raw = raw_ref[...].astype(jnp.float32)
    power = jnp.mean(raw * raw, axis=1, keepdims=True)
    factor = lax.rsqrt(power + 1e-05)
    gain = gain_ref[...]
    out_ref[:, :freqs] = (raw[:, :freqs] * factor * gain).astype(jnp.bfloat16)
    out_ref[:, freqs:] = (raw[:, freqs:] * factor * gain).astype(jnp.bfloat16)


def rotate_into(out_ref, row, source, table_ref, shift):
    rows, width = source.shape
    freqs = width // 2
    if shift == 0:
        out_ref[row : row + rows, :] = source[...]
        return
    for start in range(0, freqs, CHUNK):
        cols = slice(start, start + CHUNK)
        high = slice(freqs + start, freqs + start + CHUNK)
        cosine, sine = phase(table_ref, shift, cols)
        real = source[:, cols].astype(jnp.float32)
        imag = source[:, high].astype(jnp.float32)
        out_ref[row : row + rows, cols] = (real * cosine - imag * sine).astype(jnp.bfloat16)
        out_ref[row : row + rows, high] = (imag * cosine + real * sine).astype(jnp.bfloat16)


def rotate_kernel(table_ref, own_ref, out_ref):
    rows = own_ref.shape[0]
    for at, shift in enumerate(SHIFTS):
        rotate_into(out_ref, at * rows, own_ref, table_ref, shift)


def main_kernel(sizes, bins_ref, lag_ref, table_ref, turned_ref, *refs):
    n_rows, n_cols, count = sizes
    own_tiles = refs[:count]
    swapped_tiles = refs[count : 2 * count]
    corr_ref, grad_ref, total_ref, col_ref, turned_col_ref = refs[2 * count :]
    n_lines = n_cols // PAIR
    n_bits = n_rows.bit_length() - 1
    block, width = own_tiles[0].shape
    freqs = width // 2
    norm = 1.0 / np.sqrt(np.float32(width))
    row = lax.axis_index("rows")
    col = lax.axis_index("cols")
    line, core = col // PAIR, col % PAIR
    first = (row * n_cols + col) * block
    ratio = n_cols // n_rows
    owner = col // ratio
    col_base = (col % ratio) * n_rows

    def place(dz, slot, plane):
        in_core = core ^ plane
        dr = jnp.where(in_core == 0, slot, reverse_bits(slot, n_bits))
        return row ^ dr, (line ^ dz) * PAIR + in_core

    for dz in range(n_lines):
        tiles, spots = [], []
        for plane, group in enumerate((own_tiles, swapped_tiles)):
            for slot in range(n_rows):
                tiles.append(group[dz * n_rows + slot])
                spots.append(place(dz, slot, plane))
        span = len(tiles) * block
        for tile, (from_row, from_col) in zip(tiles, spots):
            inside = (from_col >= col_base) & (from_col < col_base + n_rows)

            @pl.when((from_row == owner) & inside)
            def _():
                start = pl.multiple_of((from_col - col_base) * block, block)
                col_ref[pl.ds(start, block), :] = tile[...]

        scores = jnp.zeros((len(SHIFTS) * block, span), jnp.float32)
        for start in range(0, width, CHUNK):
            cols = slice(start, start + CHUNK)
            stacked = jnp.concatenate([tile[:, cols] for tile in tiles], axis=0)
            scores += lax.dot_general(turned_ref[:, cols], stacked, NT, preferred_element_type=jnp.float32)
        scores = scores * norm
        lane = lax.broadcasted_iota(jnp.int32, (block, span), 1)
        mine = first + lax.broadcasted_iota(jnp.int32, (block, span), 0)
        other = jnp.zeros((block, span), jnp.int32)
        for at, (from_row, from_col) in enumerate(spots):
            base = (from_row * n_cols + from_col) * block - at * block
            other = jnp.where(lane >= at * block, base + lane, other)
        distance = jnp.abs(mine - other) // BIN
        chosen = distance == bins_ref[0]
        for entry in range(1, bins_ref.shape[0]):
            chosen = chosen | (distance == bins_ref[entry])
        selected = chosen.astype(jnp.float32)
        weights = []
        for at, shift in enumerate(SHIFTS):
            factor = 0.0
            for lag, lag_shift in enumerate(LAG_SHIFTS):
                for sign in (1, -1):
                    if sign * lag_shift == shift:
                        factor = factor + lag_ref[lag]
            part = scores[at * block : (at + 1) * block, :]
            weights.append((factor * selected * part).astype(jnp.bfloat16))
        weights = jnp.concatenate(weights, axis=0)
        for start in range(0, width, CHUNK):
            cols = slice(start, start + CHUNK)
            stacked = jnp.concatenate([tile[:, cols] for tile in tiles], axis=0)
            term = jnp.dot(weights, stacked, preferred_element_type=jnp.float32)
            if dz == 0:
                total_ref[:, cols] = term
            else:
                total_ref[:, cols] += term

    for start in range(0, freqs, CHUNK):
        cols = slice(start, start + CHUNK)
        high = slice(freqs + start, freqs + start + CHUNK)
        real_sum = jnp.zeros((block, CHUNK), jnp.float32)
        imag_sum = jnp.zeros((block, CHUNK), jnp.float32)
        for at, shift in enumerate(SHIFTS):
            real = total_ref[at * block : (at + 1) * block, cols]
            imag = total_ref[at * block : (at + 1) * block, high]
            if shift == 0:
                real_sum, imag_sum = real_sum + real, imag_sum + imag
            else:
                cosine, sine = phase(table_ref, shift, cols)
                real_sum += real * cosine + imag * sine
                imag_sum += imag * cosine - real * sine
        grad_ref[:, cols] = real_sum * norm
        grad_ref[:, high] = imag_sum * norm

    n_col = col_ref.shape[0]
    for lag, shift in enumerate(LAG_SHIFTS):
        rotate_into(turned_col_ref, lag * n_col, col_ref, table_ref, -shift)
    for plane, group in enumerate((own_tiles, swapped_tiles)):
        for dz in range(n_lines):
            _, from_col = place(dz, 0, plane)
            spot = pl.multiple_of(from_col * block, block)
            part = lax.dot_general(
                group[dz * n_rows][...], turned_col_ref[...], NT, preferred_element_type=jnp.float32
            )
            for lag in range(LAGS):
                corr_ref[lag, pl.ds(spot, block), :] = part[:, lag * n_col : (lag + 1) * n_col] * norm


def per_device(spectra, band_weights, lag_weights, selected_bins):
    n_rows = lax.axis_size("rows")
    n_cols = lax.axis_size("cols")
    n_lines = n_cols // PAIR
    n_bits = n_rows.bit_length() - 1
    block, width = spectra.shape
    freqs = width // 2
    vmem = pl.BlockSpec(memory_space=pltpu.VMEM)
    smem = pl.BlockSpec(memory_space=pltpu.SMEM)
    table = phase_table(freqs)

    def send(value, move):
        pairs = []
        for r in range(n_rows):
            for c in range(n_cols):
                to_row, to_line, to_core = move(r, c // PAIR, c % PAIR)
                pairs.append((r * n_cols + c, to_row * n_cols + to_line * PAIR + to_core))
        return lax.ppermute(value, ("rows", "cols"), pairs)

    def send_row(value, bit):
        return send(value, lambda r, z, k: (r ^ (1 << (bit if k == 0 else n_bits - 1 - bit)), z, k))

    def send_line(value, step):
        return send(value, lambda r, z, k: (r, z ^ step, k))

    def swap(value):
        return send(value, lambda r, z, k: (r, z, k ^ 1))

    whitened = pl.pallas_call(
        whiten_kernel,
        out_shape=jax.ShapeDtypeStruct((block, width), jnp.bfloat16),
        in_specs=[vmem, vmem],
        out_specs=vmem,
    )(spectra, band_weights[None, :])
    lines = [whitened]
    for dz in range(1, n_lines):
        low = dz & -dz
        lines.append(send_line(lines[dz ^ low], low))
    tiles = []
    for dz in range(n_lines):
        group = [lines[dz]]
        for slot in range(1, n_rows):
            high = slot.bit_length() - 1
            group.append(send_row(group[slot ^ (1 << high)], high))
        tiles += group
    swapped = [swap(tile) for tile in tiles]
    turned = pl.pallas_call(
        rotate_kernel,
        out_shape=jax.ShapeDtypeStruct((len(SHIFTS) * block, width), jnp.bfloat16),
        in_specs=[vmem, vmem],
        out_specs=vmem,
    )(table, whitened)
    count = len(tiles)
    n_row, n_col = n_cols * block, n_rows * block
    correlations, gradient = pl.pallas_call(
        functools.partial(main_kernel, (n_rows, n_cols, count)),
        out_shape=(
            jax.ShapeDtypeStruct((LAGS, n_row, n_col), jnp.float32),
            jax.ShapeDtypeStruct((block, width), jnp.float32),
        ),
        in_specs=[smem, smem, vmem, vmem] + [vmem] * (2 * count),
        out_specs=(vmem, vmem),
        scratch_shapes=[
            pltpu.VMEM((len(SHIFTS) * block, width), jnp.float32),
            pltpu.VMEM((n_col, width), jnp.bfloat16),
            pltpu.VMEM((LAGS * n_col, width), jnp.bfloat16),
        ],
    )(selected_bins, lag_weights, table, turned, *tiles, *swapped)
    return correlations, gradient


def solution(mesh):
    placed = (P(("rows", "cols"), None), P(), P(), P())
    return jax.shard_map(
        per_device,
        mesh=mesh,
        in_specs=placed,
        out_specs=(P(None, "rows", "cols"), P(("rows", "cols"), None)),
        check_vma=False,
    )
```

```python
import functools
import numpy as np
import jax
import jax.numpy as jnp
from jax import lax
from jax.experimental import pallas as pl
from jax.experimental.pallas import tpu as pltpu
from jax.sharding import PartitionSpec as P


LAGS = 4
LAG_STEP = 8
BIN = 128
PAIR = 2
CHUNK = 512

LAG_SHIFTS = [(lag - LAGS // 2) * LAG_STEP for lag in range(LAGS)]
SHIFTS = sorted({s for t in LAG_SHIFTS for s in (t, -t)})
TABLE = sorted({abs(s) for s in SHIFTS if s != 0})

NT = (((1,), (1,)), ((), ()))


def phase_table(freqs):
    index = np.arange(freqs, dtype=np.float64)
    rows = []
    for shift in TABLE:
        theta = np.pi * index * shift / freqs
        rows += [np.cos(theta), np.sin(theta)]
    return jnp.asarray(np.stack(rows), jnp.float32)


def phase(table_ref, shift, cols):
    at = TABLE.index(abs(shift))
    cosine = table_ref[2 * at : 2 * at + 1, cols]
    sine = table_ref[2 * at + 1 : 2 * at + 2, cols]
    return cosine, (sine if shift > 0 else -sine)


def reverse_bits(value, n_bits):
    return sum(((value >> b) & 1) << (n_bits - 1 - b) for b in range(n_bits))


def whiten_kernel(raw_ref, gain_ref, out_ref):
    freqs = gain_ref.shape[1]
    raw = raw_ref[...].astype(jnp.float32)
    power = jnp.mean(raw * raw, axis=1, keepdims=True)
    factor = lax.rsqrt(power + 1e-05)
    gain = gain_ref[...]
    out_ref[:, :freqs] = (raw[:, :freqs] * factor * gain).astype(jnp.bfloat16)
    out_ref[:, freqs:] = (raw[:, freqs:] * factor * gain).astype(jnp.bfloat16)


def rotate_into(out_ref, row, source, table_ref, shift):
    rows, width = source.shape
    freqs = width // 2
    if shift == 0:
        out_ref[row : row + rows, :] = source[...]
        return
    for start in range(0, freqs, CHUNK):
        cols = slice(start, start + CHUNK)
        high = slice(freqs + start, freqs + start + CHUNK)
        cosine, sine = phase(table_ref, shift, cols)
        real = source[:, cols].astype(jnp.float32)
        imag = source[:, high].astype(jnp.float32)
        out_ref[row : row + rows, cols] = (real * cosine - imag * sine).astype(jnp.bfloat16)
        out_ref[row : row + rows, high] = (imag * cosine + real * sine).astype(jnp.bfloat16)


def rotate_kernel(table_ref, own_ref, out_ref):
    rows = own_ref.shape[0]
    for at, shift in enumerate(SHIFTS):
        rotate_into(out_ref, at * rows, own_ref, table_ref, shift)


class Place:
    def __init__(self, n_rows, n_cols, block):
        self.n_rows, self.n_cols, self.block = n_rows, n_cols, block
        self.n_bits = n_rows.bit_length() - 1
        self.row = lax.axis_index("rows")
        self.col = lax.axis_index("cols")
        self.line, self.core = self.col // PAIR, self.col % PAIR
        self.first = (self.row * n_cols + self.col) * block
        ratio = n_cols // n_rows
        self.owner = self.col // ratio
        self.col_base = (self.col % ratio) * n_rows

    def inside(self, dz):
        from_col = (self.line ^ dz) * PAIR
        return (from_col >= self.col_base) & (from_col < self.col_base + self.n_rows)

    def half(self, dz):
        return ((self.line ^ dz) * PAIR - self.col_base) // PAIR

    def of(self, dz, slot, plane):
        in_core = self.core ^ plane
        dr = jnp.where(in_core == 0, slot, reverse_bits(slot, self.n_bits))
        return self.row ^ dr, (self.line ^ dz) * PAIR + in_core


def gather_weights(place, dz, scores, bins_ref, lag_ref):
    block = place.block
    span = scores.shape[1]
    lane = lax.broadcasted_iota(jnp.int32, (block, span), 1)
    mine = place.first + lax.broadcasted_iota(jnp.int32, (block, span), 0)
    other = jnp.zeros((block, span), jnp.int32)
    spots = [place.of(dz, slot, plane) for plane in range(PAIR) for slot in range(place.n_rows)]
    for at, (from_row, from_col) in enumerate(spots):
        base = (from_row * place.n_cols + from_col) * block - at * block
        other = jnp.where(lane >= at * block, base + lane, other)
    distance = jnp.abs(mine - other) // BIN
    chosen = distance == bins_ref[0]
    for entry in range(1, bins_ref.shape[0]):
        chosen = chosen | (distance == bins_ref[entry])
    selected = chosen.astype(jnp.float32)
    weights = []
    for at, shift in enumerate(SHIFTS):
        factor = 0.0
        for lag, lag_shift in enumerate(LAG_SHIFTS):
            for sign in (1, -1):
                if sign * lag_shift == shift:
                    factor = factor + lag_ref[lag]
        part = scores[at * block : (at + 1) * block, :]
        weights.append((factor * selected * part).astype(jnp.bfloat16))
    return jnp.concatenate(weights, axis=0)


def stack(tiles, cols):
    return jnp.concatenate([tile[:, cols] for tile in tiles], axis=0)


def bundle_step(place, dz, tiles, bins_ref, lag_ref, turned_ref, old_ref, new_ref):
    width = tiles[0].shape[1]
    norm = 1.0 / np.sqrt(np.float32(width))
    scores = jnp.zeros((turned_ref.shape[0], len(tiles) * place.block), jnp.float32)
    for start in range(0, width, CHUNK):
        cols = slice(start, start + CHUNK)
        scores += lax.dot_general(
            turned_ref[:, cols], stack(tiles, cols), NT, preferred_element_type=jnp.float32
        )
    weights = gather_weights(place, dz, scores * norm, bins_ref, lag_ref)
    for start in range(0, width, CHUNK):
        cols = slice(start, start + CHUNK)
        term = jnp.dot(weights, stack(tiles, cols), preferred_element_type=jnp.float32)
        new_ref[:, cols] = term if old_ref is None else old_ref[:, cols] + term


def pick_step(place, dz, tiles, table_ref, staged_ref, picked_ref):
    block, n_rows = place.block, place.n_rows

    @pl.when(place.inside(dz))
    def _():
        for plane in range(PAIR):
            for slot in range(n_rows):
                from_row, from_col = place.of(dz, slot, plane)
                start = pl.multiple_of((from_col % PAIR) * block, block)

                @pl.when(from_row == place.owner)
                def _():
                    staged_ref[pl.ds(start, block), :] = tiles[plane * n_rows + slot][...]

        for lag, shift in enumerate(LAG_SHIFTS):
            rotate_into(picked_ref, lag * PAIR * block, staged_ref, table_ref, -shift)


def corr_step(place, dz, lines, picked_ref, part_ref):
    block = place.block

    @pl.when(place.inside(dz))
    def _():
        for at, tile in enumerate(lines):
            _, from_col = place.of(at // PAIR, 0, at % PAIR)
            spot = pl.multiple_of(from_col * block, block)
            part_ref[pl.ds(place.half(dz), 1), pl.ds(spot, block), :] = lax.dot_general(
                tile[...], picked_ref[...], NT, preferred_element_type=jnp.float32
            )[None]


def bundle_kernel(sizes, dz, fresh, bins_ref, lag_ref, table_ref, turned_ref, *refs):
    n_rows, n_cols = sizes
    tiles = refs[: PAIR * n_rows]
    total_ref, picked_ref, staged_ref = refs[-3:]
    place = Place(n_rows, n_cols, tiles[0].shape[0])
    pick_step(place, dz, tiles, table_ref, staged_ref, picked_ref)
    old_ref = None if fresh else refs[PAIR * n_rows]
    bundle_step(place, dz, tiles, bins_ref, lag_ref, turned_ref, old_ref, total_ref)


def corr_kernel(sizes, *refs):
    n_rows, n_cols = sizes
    lines, picked, part_ref = refs[:n_cols], refs[n_cols:-1], refs[-1]
    place = Place(n_rows, n_cols, lines[0].shape[0])
    for dz, picked_ref in enumerate(picked):
        corr_step(place, dz, lines, picked_ref, part_ref)


def end_kernel(sizes, dz, bins_ref, lag_ref, table_ref, turned_ref, *refs):
    n_rows, n_cols = sizes
    count = PAIR * n_rows
    tiles, lines = refs[:count], refs[count : count + n_cols]
    old_ref, old_part_ref, corr_ref, grad_ref, total_ref, staged_ref, picked_ref, part_ref = refs[count + n_cols :]
    block, width = tiles[0].shape
    freqs = width // 2
    norm = 1.0 / np.sqrt(np.float32(width))
    place = Place(n_rows, n_cols, block)
    bundle_step(place, dz, tiles, bins_ref, lag_ref, turned_ref, old_ref, total_ref)

    for start in range(0, freqs, CHUNK):
        cols = slice(start, start + CHUNK)
        high = slice(freqs + start, freqs + start + CHUNK)
        real_sum = jnp.zeros((block, CHUNK), jnp.float32)
        imag_sum = jnp.zeros((block, CHUNK), jnp.float32)
        for at, shift in enumerate(SHIFTS):
            real = total_ref[at * block : (at + 1) * block, cols]
            imag = total_ref[at * block : (at + 1) * block, high]
            if shift == 0:
                real_sum, imag_sum = real_sum + real, imag_sum + imag
            else:
                cosine, sine = phase(table_ref, shift, cols)
                real_sum += real * cosine + imag * sine
                imag_sum += imag * cosine - real * sine
        grad_ref[:, cols] = real_sum * norm
        grad_ref[:, high] = imag_sum * norm

    pick_step(place, dz, tiles, table_ref, staged_ref, picked_ref)
    corr_step(place, dz, lines, picked_ref, part_ref)
    here = place.inside(dz)
    wide = PAIR * block
    for lag in range(LAGS):
        cols = slice(lag * wide, (lag + 1) * wide)
        halves = []
        for half in range(part_ref.shape[0]):
            fresh = here & (place.half(dz) == half)
            halves.append(jnp.where(fresh, part_ref[half, :, cols], old_part_ref[half, :, cols]))
        corr_ref[lag] = jnp.concatenate(halves, axis=1) * norm


def per_device(spectra, band_weights, lag_weights, selected_bins):
    n_rows = lax.axis_size("rows")
    n_cols = lax.axis_size("cols")
    n_lines = n_cols // PAIR
    n_bits = n_rows.bit_length() - 1
    block, width = spectra.shape
    freqs = width // 2
    vmem = pl.BlockSpec(memory_space=pltpu.VMEM)
    smem = pl.BlockSpec(memory_space=pltpu.SMEM)
    table = phase_table(freqs)

    def send(value, move):
        pairs = []
        for r in range(n_rows):
            for c in range(n_cols):
                to_row, to_line, to_core = move(r, c // PAIR, c % PAIR)
                pairs.append((r * n_cols + c, to_row * n_cols + to_line * PAIR + to_core))
        return lax.ppermute(value, ("rows", "cols"), pairs)

    def send_row(value, bit):
        return send(value, lambda r, z, k: (r ^ (1 << (bit if k == 0 else n_bits - 1 - bit)), z, k))

    def send_line(value, step):
        return send(value, lambda r, z, k: (r, z ^ step, k))

    def call(kernel, outs, operands, specs, limit, **more):
        return pl.pallas_call(
            kernel,
            out_shape=outs,
            in_specs=specs,
            out_specs=jax.tree.map(lambda _: vmem, outs),
            compiler_params=pltpu.CompilerParams(vmem_limit_bytes=limit << 20),
            **more,
        )(*operands)

    def shape(rows, dtype, *last):
        return jax.ShapeDtypeStruct((rows, *(last or (width,))), dtype)

    whitened = call(
        whiten_kernel, shape(block, jnp.bfloat16), (spectra, band_weights[None, :]), [vmem] * 2, 4
    )
    turned = call(
        rotate_kernel, shape(len(SHIFTS) * block, jnp.bfloat16), (table, whitened), [vmem] * 2, 8
    )
    lines = [whitened]
    for dz in range(1, n_lines):
        low = dz & -dz
        lines.append(send_line(lines[dz ^ low], low))
    groups = []
    for dz in range(n_lines):
        group = [lines[dz]]
        for slot in range(1, n_rows):
            if dz % 2 and slot == n_rows - 1:
                group.append(send_line(groups[dz ^ 1][slot], 1))
            else:
                high = slot.bit_length() - 1
                group.append(send_row(group[slot ^ (1 << high)], high))
        groups.append(group)
    swapped = [[send(tile, lambda r, z, k: (r, z, k ^ 1)) for tile in group] for group in groups]
    n_row, n_col = n_cols * block, n_rows * block
    sizes = (n_rows, n_cols)
    total = shape(len(SHIFTS) * block, jnp.float32)
    picked_shape = shape(LAGS * PAIR * block, jnp.bfloat16)
    staged = pltpu.VMEM((PAIR * block, width), jnp.bfloat16)
    part_shape = (n_rows // PAIR, n_row, LAGS * PAIR * block)
    state, picked = [], []
    for dz in range(n_lines - 1):
        operands = [selected_bins, lag_weights, table, turned, *groups[dz], *swapped[dz]]
        base = len(operands)
        operands += state
        new_state, new_picked = call(
            functools.partial(bundle_kernel, sizes, dz, not state),
            (total, picked_shape),
            operands,
            [smem] * 2 + [vmem] * (len(operands) - 2),
            20,
            scratch_shapes=[staged],
            input_output_aliases={base: 0} if state else {},
        )
        state = [new_state]
        picked.append(new_picked)
    last = n_lines - 1
    lines = [pair[dz][0] for dz in range(n_lines) for pair in (groups, swapped)]
    parts = call(
        functools.partial(corr_kernel, sizes),
        shape(part_shape[0], jnp.float32, *part_shape[1:]),
        [*lines, *picked],
        [vmem] * (n_cols + n_lines - 1),
        20 if n_lines <= n_rows else 40,
    )
    operands = [selected_bins, lag_weights, table, turned, *groups[last], *swapped[last], *lines, *state, parts]
    correlations, gradient = call(
        functools.partial(end_kernel, sizes, last),
        (shape(LAGS, jnp.float32, n_row, n_col), shape(block, jnp.float32)),
        operands,
        [smem] * 2 + [vmem] * (len(operands) - 2),
        36,
        scratch_shapes=[
            pltpu.VMEM(total.shape, total.dtype),
            staged,
            pltpu.VMEM(picked_shape.shape, picked_shape.dtype),
            pltpu.VMEM(part_shape, jnp.float32),
        ],
    )
    return correlations, gradient


def solution(mesh):
    placed = (P(("rows", "cols"), None), P(), P(), P())
    return jax.shard_map(
        per_device,
        mesh=mesh,
        in_specs=placed,
        out_specs=(P(None, "rows", "cols"), P(("rows", "cols"), None)),
        check_vma=False,
    )
```

```python
import functools
import numpy as np
import jax
import jax.numpy as jnp
from jax import lax
from jax.experimental import pallas as pl
from jax.experimental.pallas import tpu as pltpu
from jax.sharding import PartitionSpec as P


LAGS = 4
LAG_STEP = 8
BIN = 128
PAIR = 2
CHUNK = 512

LAG_SHIFTS = [(lag - LAGS // 2) * LAG_STEP for lag in range(LAGS)]
SHIFTS = sorted({s for t in LAG_SHIFTS for s in (t, -t)})
TABLE = sorted({abs(s) for s in SHIFTS if s != 0})

NT = (((1,), (1,)), ((), ()))


def phase_table(freqs):
    index = np.arange(freqs, dtype=np.float64)
    rows = []
    for shift in TABLE:
        theta = np.pi * index * shift / freqs
        rows += [np.cos(theta), np.sin(theta)]
    return jnp.asarray(np.stack(rows), jnp.float32)


def phase(table_ref, shift, cols):
    at = TABLE.index(abs(shift))
    cosine = table_ref[2 * at : 2 * at + 1, cols]
    sine = table_ref[2 * at + 1 : 2 * at + 2, cols]
    return cosine, (sine if shift > 0 else -sine)


def reverse_bits(value, n_bits):
    return sum(((value >> b) & 1) << (n_bits - 1 - b) for b in range(n_bits))


def whiten_kernel(raw_hbm, gain_hbm, out_ref, raw_ref, gain_ref, sems):
    copies = [
        pltpu.make_async_copy(raw_hbm, raw_ref, sems.at[0]),
        pltpu.make_async_copy(gain_hbm, gain_ref, sems.at[1]),
    ]
    for copy in copies:
        copy.start()
    for copy in copies:
        copy.wait()
    freqs = gain_ref.shape[1]
    raw = raw_ref[...].astype(jnp.float32)
    power = jnp.mean(raw * raw, axis=1, keepdims=True)
    factor = lax.rsqrt(power + 1e-05)
    gain = gain_ref[...]
    out_ref[:, :freqs] = (raw[:, :freqs] * factor * gain).astype(jnp.bfloat16)
    out_ref[:, freqs:] = (raw[:, freqs:] * factor * gain).astype(jnp.bfloat16)


def rotate_into(out_ref, row, source, table_ref, shift):
    rows, width = source.shape
    freqs = width // 2
    if shift == 0:
        out_ref[row : row + rows, :] = source[...]
        return
    for start in range(0, freqs, CHUNK):
        cols = slice(start, start + CHUNK)
        high = slice(freqs + start, freqs + start + CHUNK)
        cosine, sine = phase(table_ref, shift, cols)
        real = source[:, cols].astype(jnp.float32)
        imag = source[:, high].astype(jnp.float32)
        out_ref[row : row + rows, cols] = (real * cosine - imag * sine).astype(jnp.bfloat16)
        out_ref[row : row + rows, high] = (imag * cosine + real * sine).astype(jnp.bfloat16)


def rotate_kernel(table_ref, own_ref, out_ref):
    rows = own_ref.shape[0]
    for at, shift in enumerate(SHIFTS):
        rotate_into(out_ref, at * rows, own_ref, table_ref, shift)


class Place:
    def __init__(self, n_rows, n_cols, block):
        self.n_rows, self.n_cols, self.block = n_rows, n_cols, block
        self.n_bits = n_rows.bit_length() - 1
        self.row = lax.axis_index("rows")
        self.col = lax.axis_index("cols")
        self.line, self.core = self.col // PAIR, self.col % PAIR
        self.first = (self.row * n_cols + self.col) * block
        ratio = n_cols // n_rows
        self.owner = self.col // ratio
        self.col_base = (self.col % ratio) * n_rows

    def inside(self, dz):
        from_col = (self.line ^ dz) * PAIR
        return (from_col >= self.col_base) & (from_col < self.col_base + self.n_rows)

    def half(self, dz):
        return ((self.line ^ dz) * PAIR - self.col_base) // PAIR

    def of(self, dz, slot, plane):
        in_core = self.core ^ plane
        dr = jnp.where(in_core == 0, slot, reverse_bits(slot, self.n_bits))
        return self.row ^ dr, (self.line ^ dz) * PAIR + in_core


def gather_weights(place, dz, scores, bins_ref, lag_ref):
    block = place.block
    span = scores.shape[1]
    lane = lax.broadcasted_iota(jnp.int32, (block, span), 1)
    mine = place.first + lax.broadcasted_iota(jnp.int32, (block, span), 0)
    other = jnp.zeros((block, span), jnp.int32)
    spots = [place.of(dz, slot, plane) for plane in range(PAIR) for slot in range(place.n_rows)]
    for at, (from_row, from_col) in enumerate(spots):
        base = (from_row * place.n_cols + from_col) * block - at * block
        other = jnp.where(lane >= at * block, base + lane, other)
    distance = jnp.abs(mine - other) // BIN
    chosen = distance == bins_ref[0]
    for entry in range(1, bins_ref.shape[0]):
        chosen = chosen | (distance == bins_ref[entry])
    selected = chosen.astype(jnp.float32)
    weights = []
    for at, shift in enumerate(SHIFTS):
        factor = 0.0
        for lag, lag_shift in enumerate(LAG_SHIFTS):
            for sign in (1, -1):
                if sign * lag_shift == shift:
                    factor = factor + lag_ref[lag]
        part = scores[at * block : (at + 1) * block, :]
        weights.append((factor * selected * part).astype(jnp.bfloat16))
    return jnp.concatenate(weights, axis=0)


def stack(tiles, cols):
    return jnp.concatenate([tile[:, cols] for tile in tiles], axis=0)


def bundle_step(place, dz, tiles, bins_ref, lag_ref, turned_ref, old_ref, new_ref):
    width = tiles[0].shape[1]
    norm = 1.0 / np.sqrt(np.float32(width))
    scores = jnp.zeros((turned_ref.shape[0], len(tiles) * place.block), jnp.float32)
    for start in range(0, width, CHUNK):
        cols = slice(start, start + CHUNK)
        scores += lax.dot_general(
            turned_ref[:, cols], stack(tiles, cols), NT, preferred_element_type=jnp.float32
        )
    weights = gather_weights(place, dz, scores * norm, bins_ref, lag_ref)
    for start in range(0, width, CHUNK):
        cols = slice(start, start + CHUNK)
        term = jnp.dot(weights, stack(tiles, cols), preferred_element_type=jnp.float32)
        new_ref[:, cols] = term if old_ref is None else old_ref[:, cols] + term


def pick_step(place, dz, tiles, table_ref, staged_ref, picked_ref):
    block, n_rows = place.block, place.n_rows

    @pl.when(place.inside(dz))
    def _():
        for plane in range(PAIR):
            for slot in range(n_rows):
                from_row, from_col = place.of(dz, slot, plane)
                start = pl.multiple_of((from_col % PAIR) * block, block)

                @pl.when(from_row == place.owner)
                def _():
                    staged_ref[pl.ds(start, block), :] = tiles[plane * n_rows + slot][...]

        for lag, shift in enumerate(LAG_SHIFTS):
            rotate_into(picked_ref, lag * PAIR * block, staged_ref, table_ref, -shift)


def corr_step(place, dz, lines, picked_ref, part_ref):
    block = place.block
    width = picked_ref.shape[1]

    @pl.when(place.inside(dz))
    def _():
        part = jnp.zeros((len(lines) * block, picked_ref.shape[0]), jnp.float32)
        for start in range(0, width, CHUNK):
            cols = slice(start, start + CHUNK)
            part += lax.dot_general(
                stack(lines, cols), picked_ref[:, cols], NT, preferred_element_type=jnp.float32
            )
        for at in range(len(lines)):
            _, from_col = place.of(at // PAIR, 0, at % PAIR)
            spot = pl.multiple_of(from_col * block, block)
            part_ref[pl.ds(place.half(dz), 1), pl.ds(spot, block), :] = part[at * block : (at + 1) * block][None]


def bundle_kernel(sizes, dz, fresh, bins_ref, lag_ref, table_ref, turned_ref, *refs):
    n_rows, n_cols = sizes
    tiles = refs[: PAIR * n_rows]
    total_ref, picked_ref, staged_ref = refs[-3:]
    place = Place(n_rows, n_cols, tiles[0].shape[0])
    pick_step(place, dz, tiles, table_ref, staged_ref, picked_ref)
    old_ref = None if fresh else refs[PAIR * n_rows]
    bundle_step(place, dz, tiles, bins_ref, lag_ref, turned_ref, old_ref, total_ref)


def corr_kernel(sizes, *refs):
    n_rows, n_cols = sizes
    lines, picked, part_ref = refs[:n_cols], refs[n_cols:-1], refs[-1]
    place = Place(n_rows, n_cols, lines[0].shape[0])
    for dz, picked_ref in enumerate(picked):
        corr_step(place, dz, lines, picked_ref, part_ref)


def end_kernel(sizes, dz, bins_ref, lag_ref, table_ref, turned_ref, *refs):
    n_rows, n_cols = sizes
    count = PAIR * n_rows
    tiles, lines = refs[:count], refs[count : count + n_cols]
    old_ref, old_part_ref, corr_ref, grad_ref, total_ref, staged_ref, picked_ref, part_ref = refs[count + n_cols :]
    block, width = tiles[0].shape
    freqs = width // 2
    norm = 1.0 / np.sqrt(np.float32(width))
    place = Place(n_rows, n_cols, block)
    bundle_step(place, dz, tiles, bins_ref, lag_ref, turned_ref, old_ref, total_ref)

    for start in range(0, freqs, CHUNK):
        cols = slice(start, start + CHUNK)
        high = slice(freqs + start, freqs + start + CHUNK)
        real_sum = jnp.zeros((block, CHUNK), jnp.float32)
        imag_sum = jnp.zeros((block, CHUNK), jnp.float32)
        for at, shift in enumerate(SHIFTS):
            real = total_ref[at * block : (at + 1) * block, cols]
            imag = total_ref[at * block : (at + 1) * block, high]
            if shift == 0:
                real_sum, imag_sum = real_sum + real, imag_sum + imag
            else:
                cosine, sine = phase(table_ref, shift, cols)
                real_sum += real * cosine + imag * sine
                imag_sum += imag * cosine - real * sine
        grad_ref[:, cols] = real_sum * norm
        grad_ref[:, high] = imag_sum * norm

    pick_step(place, dz, tiles, table_ref, staged_ref, picked_ref)
    corr_step(place, dz, lines, picked_ref, part_ref)
    here = place.inside(dz)
    wide = PAIR * block
    for lag in range(LAGS):
        cols = slice(lag * wide, (lag + 1) * wide)
        halves = []
        for half in range(part_ref.shape[0]):
            fresh = here & (place.half(dz) == half)
            halves.append(jnp.where(fresh, part_ref[half, :, cols], old_part_ref[half, :, cols]))
        corr_ref[lag] = jnp.concatenate(halves, axis=1) * norm


def per_device(spectra, band_weights, lag_weights, selected_bins):
    n_rows = lax.axis_size("rows")
    n_cols = lax.axis_size("cols")
    n_lines = n_cols // PAIR
    n_bits = n_rows.bit_length() - 1
    block, width = spectra.shape
    freqs = width // 2
    vmem = pl.BlockSpec(memory_space=pltpu.VMEM)
    smem = pl.BlockSpec(memory_space=pltpu.SMEM)
    table = phase_table(freqs)

    def send(value, move):
        pairs = []
        for r in range(n_rows):
            for c in range(n_cols):
                to_row, to_line, to_core = move(r, c // PAIR, c % PAIR)
                pairs.append((r * n_cols + c, to_row * n_cols + to_line * PAIR + to_core))
        return lax.ppermute(value, ("rows", "cols"), pairs)

    def send_row(value, bit):
        return send(value, lambda r, z, k: (r ^ (1 << (bit if k == 0 else n_bits - 1 - bit)), z, k))

    def send_line(value, step):
        return send(value, lambda r, z, k: (r, z ^ step, k))

    def call(kernel, outs, operands, specs, limit, **more):
        return pl.pallas_call(
            kernel,
            out_shape=outs,
            in_specs=specs,
            out_specs=jax.tree.map(lambda _: vmem, outs),
            compiler_params=pltpu.CompilerParams(vmem_limit_bytes=limit << 20),
            **more,
        )(*operands)

    def shape(rows, dtype, *last):
        return jax.ShapeDtypeStruct((rows, *(last or (width,))), dtype)

    whitened = call(
        whiten_kernel,
        shape(block, jnp.bfloat16),
        (spectra, band_weights[None, :]),
        [pl.BlockSpec(memory_space=pltpu.HBM)] * 2,
        4,
        scratch_shapes=[
            pltpu.VMEM((block, width), spectra.dtype),
            pltpu.VMEM((1, freqs), jnp.float32),
            pltpu.SemaphoreType.DMA((2,)),
        ],
    )
    turned = call(
        rotate_kernel, shape(len(SHIFTS) * block, jnp.bfloat16), (table, whitened), [vmem] * 2, 8
    )
    lines = [whitened]
    for dz in range(1, n_lines):
        low = dz & -dz
        lines.append(send_line(lines[dz ^ low], low))
    groups = []
    for dz in range(n_lines):
        group = [lines[dz]]
        for slot in range(1, n_rows):
            if dz % 2 and slot == n_rows - 1:
                group.append(send_line(groups[dz ^ 1][slot], 1))
            else:
                high = slot.bit_length() - 1
                group.append(send_row(group[slot ^ (1 << high)], high))
        groups.append(group)
    swapped = [[send(tile, lambda r, z, k: (r, z, k ^ 1)) for tile in group] for group in groups]
    n_row, n_col = n_cols * block, n_rows * block
    sizes = (n_rows, n_cols)
    total = shape(len(SHIFTS) * block, jnp.float32)
    picked_shape = shape(LAGS * PAIR * block, jnp.bfloat16)
    staged = pltpu.VMEM((PAIR * block, width), jnp.bfloat16)
    part_shape = (n_rows // PAIR, n_row, LAGS * PAIR * block)
    state, picked = [], []
    for dz in range(n_lines - 1):
        operands = [selected_bins, lag_weights, table, turned, *groups[dz], *swapped[dz]]
        base = len(operands)
        operands += state
        new_state, new_picked = call(
            functools.partial(bundle_kernel, sizes, dz, not state),
            (total, picked_shape),
            operands,
            [smem] * 2 + [vmem] * (len(operands) - 2),
            20,
            scratch_shapes=[staged],
            input_output_aliases={base: 0} if state else {},
        )
        state = [new_state]
        picked.append(new_picked)
    last = n_lines - 1
    lines = [pair[dz][0] for dz in range(n_lines) for pair in (groups, swapped)]
    parts = call(
        functools.partial(corr_kernel, sizes),
        shape(part_shape[0], jnp.float32, *part_shape[1:]),
        [*lines, *picked],
        [vmem] * (n_cols + n_lines - 1),
        20 if n_lines <= n_rows else 40,
    )
    operands = [selected_bins, lag_weights, table, turned, *groups[last], *swapped[last], *lines, *state, parts]
    correlations, gradient = call(
        functools.partial(end_kernel, sizes, last),
        (shape(LAGS, jnp.float32, n_row, n_col), shape(block, jnp.float32)),
        operands,
        [smem] * 2 + [vmem] * (len(operands) - 2),
        36,
        scratch_shapes=[
            pltpu.VMEM(total.shape, total.dtype),
            staged,
            pltpu.VMEM(picked_shape.shape, picked_shape.dtype),
            pltpu.VMEM(part_shape, jnp.float32),
        ],
    )
    return correlations, gradient


def solution(mesh):
    placed = (P(("rows", "cols"), None), P(), P(), P())
    return jax.shard_map(
        per_device,
        mesh=mesh,
        in_specs=placed,
        out_specs=(P(None, "rows", "cols"), P(("rows", "cols"), None)),
        check_vma=False,
    )
```

```python
import functools
import numpy as np
import jax
import jax.numpy as jnp
from jax import lax
from jax.experimental import pallas as pl
from jax.experimental.pallas import tpu as pltpu
from jax.sharding import PartitionSpec as P


LAGS = 4
LAG_STEP = 8
BIN = 128
PAIR = 2
CHUNK = 512

LAG_SHIFTS = [(lag - LAGS // 2) * LAG_STEP for lag in range(LAGS)]
SHIFTS = sorted({s for t in LAG_SHIFTS for s in (t, -t)})
TABLE = sorted({abs(s) for s in SHIFTS if s != 0})

NT = (((1,), (1,)), ((), ()))


def phase_table(freqs):
    index = np.arange(freqs, dtype=np.float64)
    rows = []
    for shift in TABLE:
        theta = np.pi * index * shift / freqs
        rows += [np.cos(theta), np.sin(theta)]
    return jnp.asarray(np.stack(rows), jnp.float32)


def phase(table_ref, shift, cols):
    at = TABLE.index(abs(shift))
    cosine = table_ref[2 * at : 2 * at + 1, cols]
    sine = table_ref[2 * at + 1 : 2 * at + 2, cols]
    return cosine, (sine if shift > 0 else -sine)


def reverse_bits(value, n_bits):
    return sum(((value >> b) & 1) << (n_bits - 1 - b) for b in range(n_bits))


def whiten_kernel(raw_hbm, gain_hbm, out_ref, raw_ref, gain_ref, sems):
    copies = [
        pltpu.make_async_copy(raw_hbm, raw_ref, sems.at[0]),
        pltpu.make_async_copy(gain_hbm, gain_ref, sems.at[1]),
    ]
    for copy in copies:
        copy.start()
    for copy in copies:
        copy.wait()
    freqs = gain_ref.shape[1]
    raw = raw_ref[...].astype(jnp.float32)
    power = jnp.mean(raw * raw, axis=1, keepdims=True)
    factor = lax.rsqrt(power + 1e-05)
    gain = gain_ref[...]
    out_ref[:, :freqs] = (raw[:, :freqs] * factor * gain).astype(jnp.bfloat16)
    out_ref[:, freqs:] = (raw[:, freqs:] * factor * gain).astype(jnp.bfloat16)


def rotate_into(out_ref, row, source, table_ref, shift):
    rows, width = source.shape
    freqs = width // 2
    if shift == 0:
        out_ref[row : row + rows, :] = source[...]
        return
    for start in range(0, freqs, CHUNK):
        cols = slice(start, start + CHUNK)
        high = slice(freqs + start, freqs + start + CHUNK)
        cosine, sine = phase(table_ref, shift, cols)
        real = source[:, cols].astype(jnp.float32)
        imag = source[:, high].astype(jnp.float32)
        out_ref[row : row + rows, cols] = (real * cosine - imag * sine).astype(jnp.bfloat16)
        out_ref[row : row + rows, high] = (imag * cosine + real * sine).astype(jnp.bfloat16)


def rotate_kernel(table_ref, own_ref, out_ref):
    rows = own_ref.shape[0]
    for at, shift in enumerate(SHIFTS):
        rotate_into(out_ref, at * rows, own_ref, table_ref, shift)


class Place:
    def __init__(self, n_rows, n_cols, block):
        self.n_rows, self.n_cols, self.block = n_rows, n_cols, block
        self.n_bits = n_rows.bit_length() - 1
        self.row = lax.axis_index("rows")
        self.col = lax.axis_index("cols")
        self.line, self.core = self.col // PAIR, self.col % PAIR
        self.first = (self.row * n_cols + self.col) * block
        ratio = n_cols // n_rows
        self.owner = self.col // ratio
        self.col_base = (self.col % ratio) * n_rows

    def inside(self, dz):
        from_col = (self.line ^ dz) * PAIR
        return (from_col >= self.col_base) & (from_col < self.col_base + self.n_rows)

    def half(self, dz):
        return ((self.line ^ dz) * PAIR - self.col_base) // PAIR

    def of(self, dz, slot, plane):
        in_core = self.core ^ plane
        dr = jnp.where(in_core == 0, slot, reverse_bits(slot, self.n_bits))
        return self.row ^ dr, (self.line ^ dz) * PAIR + in_core


def gather_weights(place, spots, scores, bins_ref, lag_ref):
    block = place.block
    span = scores.shape[1]
    lane = lax.broadcasted_iota(jnp.int32, (block, span), 1)
    mine = place.first + lax.broadcasted_iota(jnp.int32, (block, span), 0)
    other = jnp.zeros((block, span), jnp.int32)
    for at, (from_row, from_col) in enumerate(spots):
        base = (from_row * place.n_cols + from_col) * block - at * block
        other = jnp.where(lane >= at * block, base + lane, other)
    distance = jnp.abs(mine - other) // BIN
    chosen = distance == bins_ref[0]
    for entry in range(1, bins_ref.shape[0]):
        chosen = chosen | (distance == bins_ref[entry])
    selected = chosen.astype(jnp.float32)
    weights = []
    for at, shift in enumerate(SHIFTS):
        factor = 0.0
        for lag, lag_shift in enumerate(LAG_SHIFTS):
            for sign in (1, -1):
                if sign * lag_shift == shift:
                    factor = factor + lag_ref[lag]
        part = scores[at * block : (at + 1) * block, :]
        weights.append((factor * selected * part).astype(jnp.bfloat16))
    return jnp.concatenate(weights, axis=0)


def stack(tiles, cols):
    return jnp.concatenate([tile[:, cols] for tile in tiles], axis=0)


def bundle_weights(place, dz, tiles, bins_ref, lag_ref, turned_ref, skip=0):
    width = tiles[0].shape[1]
    norm = 1.0 / np.sqrt(np.float32(width))
    scores = jnp.zeros((turned_ref.shape[0], len(tiles) * place.block), jnp.float32)
    for start in range(0, width, CHUNK):
        cols = slice(start, start + CHUNK)
        scores += lax.dot_general(
            turned_ref[:, cols], stack(tiles, cols), NT, preferred_element_type=jnp.float32
        )
    spots = [place.of(dz, slot, plane) for plane in range(PAIR) for slot in range(place.n_rows)]
    return gather_weights(place, spots[skip : skip + len(tiles)], scores * norm, bins_ref, lag_ref)


def pick_step(place, dz, tiles, table_ref, staged_ref, picked_ref):
    block, n_rows = place.block, place.n_rows

    @pl.when(place.inside(dz))
    def _():
        for plane in range(PAIR):
            for slot in range(n_rows):
                from_row, from_col = place.of(dz, slot, plane)
                start = pl.multiple_of((from_col % PAIR) * block, block)

                @pl.when(from_row == place.owner)
                def _():
                    staged_ref[pl.ds(start, block), :] = tiles[plane * n_rows + slot][...]

        for lag, shift in enumerate(LAG_SHIFTS):
            rotate_into(picked_ref, lag * PAIR * block, staged_ref, table_ref, -shift)


def corr_step(place, dz, lines, picked_ref, part_ref):
    block = place.block
    width = picked_ref.shape[1]

    @pl.when(place.inside(dz))
    def _():
        part = jnp.zeros((len(lines) * block, picked_ref.shape[0]), jnp.float32)
        for start in range(0, width, CHUNK):
            cols = slice(start, start + CHUNK)
            part += lax.dot_general(
                stack(lines, cols), picked_ref[:, cols], NT, preferred_element_type=jnp.float32
            )
        for at in range(len(lines)):
            _, from_col = place.of(at // PAIR, 0, at % PAIR)
            spot = pl.multiple_of(from_col * block, block)
            part_ref[pl.ds(place.half(dz), 1), pl.ds(spot, block), :] = part[at * block : (at + 1) * block][None]


def bundle_kernel(sizes, dz, bins_ref, lag_ref, table_ref, turned_ref, *refs):
    n_rows, n_cols = sizes
    weights_ref, picked_ref, staged_ref = refs[-3:]
    tiles = refs[:-3]
    place = Place(n_rows, n_cols, tiles[0].shape[0])
    pick_step(place, dz, tiles, table_ref, staged_ref, picked_ref)
    weights_ref[...] = bundle_weights(place, dz, tiles, bins_ref, lag_ref, turned_ref)


def partial_kernel(sizes, dz, bins_ref, lag_ref, turned_ref, *refs):
    tiles, weights_ref = refs[:-1], refs[-1]
    place = Place(*sizes, tiles[0].shape[0])
    weights_ref[...] = bundle_weights(place, dz, tiles, bins_ref, lag_ref, turned_ref)


def corr_kernel(sizes, *refs):
    n_rows, n_cols = sizes
    lines, picked, part_ref = refs[:n_cols], refs[n_cols:-1], refs[-1]
    place = Place(n_rows, n_cols, lines[0].shape[0])
    for dz, picked_ref in enumerate(picked):
        corr_step(place, dz, lines, picked_ref, part_ref)


def end_kernel(sizes, dz, bins_ref, lag_ref, table_ref, turned_ref, *refs):
    n_rows, n_cols = sizes
    per_line = PAIR * n_rows
    count = (n_cols // PAIR) * per_line
    every, old_weights = refs[:count], refs[count : count + dz + 1]
    old_part_ref, corr_ref, grad_ref, weights_ref, staged_ref, picked_ref, part_ref = refs[count + dz + 1 :]
    tiles = every[dz * per_line :]
    lines = every[::n_rows]
    block, width = tiles[0].shape
    freqs = width // 2
    norm = 1.0 / np.sqrt(np.float32(width))
    place = Place(n_rows, n_cols, block)
    span = per_line * block
    fresh = bundle_weights(place, dz, tiles[-1:], bins_ref, lag_ref, turned_ref, per_line - 1)
    for at, old_ref in enumerate(old_weights[:-1]):
        weights_ref[:, at * span : (at + 1) * span] = old_ref[...]
    weights_ref[:, dz * span :] = jnp.concatenate([old_weights[-1][...], fresh], axis=1)

    for start in range(0, freqs, CHUNK):
        cols = slice(start, start + CHUNK)
        high = slice(freqs + start, freqs + start + CHUNK)
        reals = jnp.dot(weights_ref[...], stack(every, cols), preferred_element_type=jnp.float32)
        imags = jnp.dot(weights_ref[...], stack(every, high), preferred_element_type=jnp.float32)
        real_sum = jnp.zeros((block, CHUNK), jnp.float32)
        imag_sum = jnp.zeros((block, CHUNK), jnp.float32)
        for at, shift in enumerate(SHIFTS):
            real = reals[at * block : (at + 1) * block]
            imag = imags[at * block : (at + 1) * block]
            if shift == 0:
                real_sum, imag_sum = real_sum + real, imag_sum + imag
            else:
                cosine, sine = phase(table_ref, shift, cols)
                real_sum += real * cosine + imag * sine
                imag_sum += imag * cosine - real * sine
        grad_ref[:, cols] = real_sum * norm
        grad_ref[:, high] = imag_sum * norm

    pick_step(place, dz, tiles, table_ref, staged_ref, picked_ref)
    corr_step(place, dz, lines, picked_ref, part_ref)
    here = place.inside(dz)
    wide = PAIR * block
    for lag in range(LAGS):
        cols = slice(lag * wide, (lag + 1) * wide)
        halves = []
        for half in range(part_ref.shape[0]):
            fresh = here & (place.half(dz) == half)
            halves.append(jnp.where(fresh, part_ref[half, :, cols], old_part_ref[half, :, cols]))
        corr_ref[lag] = jnp.concatenate(halves, axis=1) * norm


def per_device(spectra, band_weights, lag_weights, selected_bins):
    n_rows = lax.axis_size("rows")
    n_cols = lax.axis_size("cols")
    n_lines = n_cols // PAIR
    n_bits = n_rows.bit_length() - 1
    block, width = spectra.shape
    freqs = width // 2
    vmem = pl.BlockSpec(memory_space=pltpu.VMEM)
    smem = pl.BlockSpec(memory_space=pltpu.SMEM)
    table = phase_table(freqs)

    def send(value, move):
        pairs = []
        for r in range(n_rows):
            for c in range(n_cols):
                to_row, to_line, to_core = move(r, c // PAIR, c % PAIR)
                pairs.append((r * n_cols + c, to_row * n_cols + to_line * PAIR + to_core))
        return lax.ppermute(value, ("rows", "cols"), pairs)

    def send_row(value, bit):
        return send(value, lambda r, z, k: (r ^ (1 << (bit if k == 0 else n_bits - 1 - bit)), z, k))

    def send_line(value, step):
        return send(value, lambda r, z, k: (r, z ^ step, k))

    def call(kernel, outs, operands, specs, **more):
        held = sum(x.size * x.dtype.itemsize for x in [*operands, *jax.tree.leaves(outs)])
        return pl.pallas_call(
            kernel,
            out_shape=outs,
            in_specs=specs,
            out_specs=jax.tree.map(lambda _: vmem, outs),
            compiler_params=pltpu.CompilerParams(vmem_limit_bytes=min(held + (12 << 20), 60 << 20)),
            **more,
        )(*operands)

    def shape(rows, dtype, *last):
        return jax.ShapeDtypeStruct((rows, *(last or (width,))), dtype)

    whitened = call(
        whiten_kernel,
        shape(block, jnp.bfloat16),
        (spectra, band_weights[None, :]),
        [pl.BlockSpec(memory_space=pltpu.HBM)] * 2,
        scratch_shapes=[
            pltpu.VMEM((block, width), spectra.dtype),
            pltpu.VMEM((1, freqs), jnp.float32),
            pltpu.SemaphoreType.DMA((2,)),
        ],
    )
    turned = call(
        rotate_kernel, shape(len(SHIFTS) * block, jnp.bfloat16), (table, whitened), [vmem] * 2
    )
    lines = [whitened]
    for dz in range(1, n_lines):
        low = dz & -dz
        lines.append(send_line(lines[dz ^ low], low))
    groups = []
    for dz in range(n_lines):
        group = [lines[dz]]
        for slot in range(1, n_rows):
            if dz % 2 and slot == n_rows - 1:
                group.append(send_line(groups[dz ^ 1][slot], 1))
            else:
                high = slot.bit_length() - 1
                group.append(send_row(group[slot ^ (1 << high)], high))
        groups.append(group)
    swapped = [[send(tile, lambda r, z, k: (r, z, k ^ 1)) for tile in group] for group in groups]
    n_row, n_col = n_cols * block, n_rows * block
    sizes = (n_rows, n_cols)
    every = [[*groups[dz], *swapped[dz]] for dz in range(n_lines)]
    weights_shape = shape(len(SHIFTS) * block, jnp.bfloat16, PAIR * n_rows * block)
    picked_shape = shape(LAGS * PAIR * block, jnp.bfloat16)
    staged = pltpu.VMEM((PAIR * block, width), jnp.bfloat16)
    part_shape = (n_rows // PAIR, n_row, LAGS * PAIR * block)
    common = [selected_bins, lag_weights, table, turned]
    weights, picked = [], []
    for dz in range(n_lines - 1):
        operands = [*common, *every[dz]]
        new_weights, new_picked = call(
            functools.partial(bundle_kernel, sizes, dz),
            (weights_shape, picked_shape),
            operands,
            [smem] * 2 + [vmem] * (len(operands) - 2),
            scratch_shapes=[staged],
        )
        weights.append(new_weights)
        picked.append(new_picked)
    last = n_lines - 1
    operands = [selected_bins, lag_weights, turned, *every[last][:-1]]
    weights.append(
        call(
            functools.partial(partial_kernel, sizes, last),
            shape(len(SHIFTS) * block, jnp.bfloat16, (PAIR * n_rows - 1) * block),
            operands,
            [smem] * 2 + [vmem] * (len(operands) - 2),
        )
    )
    lines = [tile for group in every for tile in group[::n_rows]]
    parts = call(
        functools.partial(corr_kernel, sizes),
        shape(part_shape[0], jnp.float32, *part_shape[1:]),
        [*lines, *picked],
        [vmem] * (n_cols + n_lines - 1),
    )
    operands = [*common, *(tile for group in every for tile in group), *weights, parts]
    correlations, gradient = call(
        functools.partial(end_kernel, sizes, n_lines - 1),
        (shape(LAGS, jnp.float32, n_row, n_col), shape(block, jnp.float32)),
        operands,
        [smem] * 2 + [vmem] * (len(operands) - 2),
        scratch_shapes=[
            pltpu.VMEM((len(SHIFTS) * block, n_rows * n_cols * block), jnp.bfloat16),
            staged,
            pltpu.VMEM(picked_shape.shape, picked_shape.dtype),
            pltpu.VMEM(part_shape, jnp.float32),
        ],
    )
    return correlations, gradient


def solution(mesh):
    placed = (P(("rows", "cols"), None), P(), P(), P())
    return jax.shard_map(
        per_device,
        mesh=mesh,
        in_specs=placed,
        out_specs=(P(None, "rows", "cols"), P(("rows", "cols"), None)),
        check_vma=False,
    )
```

```python
import functools
import numpy as np
import jax
import jax.numpy as jnp
from jax import lax
from jax.experimental import pallas as pl
from jax.experimental.pallas import tpu as pltpu
from jax.sharding import PartitionSpec as P


LAGS = 4
LAG_STEP = 8
BIN = 128
PAIR = 2
CHUNK = 512

LAG_SHIFTS = [(lag - LAGS // 2) * LAG_STEP for lag in range(LAGS)]
SHIFTS = sorted({s for t in LAG_SHIFTS for s in (t, -t)})
TABLE = sorted({abs(s) for s in SHIFTS if s != 0})

NT = (((1,), (1,)), ((), ()))


def phase_table(freqs):
    index = np.arange(freqs, dtype=np.float64)
    rows = []
    for shift in TABLE:
        theta = np.pi * index * shift / freqs
        rows += [np.cos(theta), np.sin(theta)]
    return jnp.asarray(np.stack(rows), jnp.float32)


def phase(table_ref, shift, cols):
    at = TABLE.index(abs(shift))
    cosine = table_ref[2 * at : 2 * at + 1, cols]
    sine = table_ref[2 * at + 1 : 2 * at + 2, cols]
    return cosine, (sine if shift > 0 else -sine)


def reverse_bits(value, n_bits):
    return sum(((value >> b) & 1) << (n_bits - 1 - b) for b in range(n_bits))


def whiten_kernel(raw_hbm, gain_hbm, out_ref, raw_ref, gain_ref, sems):
    copies = [
        pltpu.make_async_copy(raw_hbm, raw_ref, sems.at[0]),
        pltpu.make_async_copy(gain_hbm, gain_ref, sems.at[1]),
    ]
    for copy in copies:
        copy.start()
    for copy in copies:
        copy.wait()
    freqs = gain_ref.shape[1]
    raw = raw_ref[...].astype(jnp.float32)
    power = jnp.mean(raw * raw, axis=1, keepdims=True)
    factor = lax.rsqrt(power + 1e-05)
    gain = gain_ref[...]
    out_ref[:, :freqs] = (raw[:, :freqs] * factor * gain).astype(jnp.bfloat16)
    out_ref[:, freqs:] = (raw[:, freqs:] * factor * gain).astype(jnp.bfloat16)


def rotate_into(out_ref, row, source, table_ref, shift):
    rows, width = source.shape
    freqs = width // 2
    if shift == 0:
        out_ref[row : row + rows, :] = source[...]
        return
    for start in range(0, freqs, CHUNK):
        cols = slice(start, start + CHUNK)
        high = slice(freqs + start, freqs + start + CHUNK)
        cosine, sine = phase(table_ref, shift, cols)
        real = source[:, cols].astype(jnp.float32)
        imag = source[:, high].astype(jnp.float32)
        out_ref[row : row + rows, cols] = (real * cosine - imag * sine).astype(jnp.bfloat16)
        out_ref[row : row + rows, high] = (imag * cosine + real * sine).astype(jnp.bfloat16)


def rotate_kernel(table_ref, own_ref, out_ref):
    rows = own_ref.shape[0]
    for at, shift in enumerate(SHIFTS):
        rotate_into(out_ref, at * rows, own_ref, table_ref, shift)


class Place:
    def __init__(self, n_rows, n_cols, block):
        self.n_rows, self.n_cols, self.block = n_rows, n_cols, block
        self.n_bits = n_rows.bit_length() - 1
        self.row = lax.axis_index("rows")
        self.col = lax.axis_index("cols")
        self.line, self.core = self.col // PAIR, self.col % PAIR
        self.first = (self.row * n_cols + self.col) * block
        ratio = n_cols // n_rows
        self.owner = self.col // ratio
        self.col_base = (self.col % ratio) * n_rows

    def inside(self, dz):
        from_col = (self.line ^ dz) * PAIR
        return (from_col >= self.col_base) & (from_col < self.col_base + self.n_rows)

    def half(self, dz):
        return ((self.line ^ dz) * PAIR - self.col_base) // PAIR

    def of(self, dz, slot, plane):
        in_core = self.core ^ plane
        dr = jnp.where(in_core == 0, slot, reverse_bits(slot, self.n_bits))
        return self.row ^ dr, (self.line ^ dz) * PAIR + in_core


def gather_weights(place, spots, scores, bins_ref, lag_ref):
    block = place.block
    span = scores.shape[1]
    lane = lax.broadcasted_iota(jnp.int32, (block, span), 1)
    mine = place.first + lax.broadcasted_iota(jnp.int32, (block, span), 0)
    other = jnp.zeros((block, span), jnp.int32)
    for at, (from_row, from_col) in enumerate(spots):
        base = (from_row * place.n_cols + from_col) * block - at * block
        other = jnp.where(lane >= at * block, base + lane, other)
    distance = jnp.abs(mine - other) // BIN
    chosen = distance == bins_ref[0]
    for entry in range(1, bins_ref.shape[0]):
        chosen = chosen | (distance == bins_ref[entry])
    selected = chosen.astype(jnp.float32)
    weights = []
    for at, shift in enumerate(SHIFTS):
        factor = 0.0
        for lag, lag_shift in enumerate(LAG_SHIFTS):
            for sign in (1, -1):
                if sign * lag_shift == shift:
                    factor = factor + lag_ref[lag]
        part = scores[at * block : (at + 1) * block, :]
        weights.append((factor * selected * part).astype(jnp.bfloat16))
    return jnp.concatenate(weights, axis=0)


def stack(tiles, cols):
    return jnp.concatenate([tile[:, cols] for tile in tiles], axis=0)


def bundle_weights(place, dz, tiles, bins_ref, lag_ref, turned_ref, skip=0):
    width = tiles[0].shape[1]
    norm = 1.0 / np.sqrt(np.float32(width))
    scores = jnp.zeros((turned_ref.shape[0], len(tiles) * place.block), jnp.float32)
    for start in range(0, width, CHUNK):
        cols = slice(start, start + CHUNK)
        scores += lax.dot_general(
            turned_ref[:, cols], stack(tiles, cols), NT, preferred_element_type=jnp.float32
        )
    spots = [place.of(dz, slot, plane) for plane in range(PAIR) for slot in range(place.n_rows)]
    return gather_weights(place, spots[skip : skip + len(tiles)], scores * norm, bins_ref, lag_ref)


def pick_step(place, dz, tiles, table_ref, staged_ref, picked_ref):
    block, n_rows = place.block, place.n_rows

    @pl.when(place.inside(dz))
    def _():
        for plane in range(PAIR):
            for slot in range(n_rows):
                from_row, from_col = place.of(dz, slot, plane)
                start = pl.multiple_of((from_col % PAIR) * block, block)

                @pl.when(from_row == place.owner)
                def _():
                    staged_ref[pl.ds(start, block), :] = tiles[plane * n_rows + slot][...]

        for lag, shift in enumerate(LAG_SHIFTS):
            rotate_into(picked_ref, lag * PAIR * block, staged_ref, table_ref, -shift)


def corr_step(place, dz, lines, picked_ref, part_ref):
    block = place.block
    width = picked_ref.shape[1]

    @pl.when(place.inside(dz))
    def _():
        part = jnp.zeros((len(lines) * block, picked_ref.shape[0]), jnp.float32)
        for start in range(0, width, CHUNK):
            cols = slice(start, start + CHUNK)
            part += lax.dot_general(
                stack(lines, cols), picked_ref[:, cols], NT, preferred_element_type=jnp.float32
            )
        for at in range(len(lines)):
            _, from_col = place.of(at // PAIR, 0, at % PAIR)
            spot = pl.multiple_of(from_col * block, block)
            part_ref[pl.ds(place.half(dz), 1), pl.ds(spot, block), :] = part[at * block : (at + 1) * block][None]


def bundle_kernel(sizes, dz, bins_ref, lag_ref, table_ref, turned_ref, *refs):
    n_rows, n_cols = sizes
    weights_ref, picked_ref, staged_ref = refs[-3:]
    tiles = refs[:-3]
    place = Place(n_rows, n_cols, tiles[0].shape[0])
    pick_step(place, dz, tiles, table_ref, staged_ref, picked_ref)
    weights_ref[...] = bundle_weights(place, dz, tiles, bins_ref, lag_ref, turned_ref)


def partial_kernel(sizes, dz, bins_ref, lag_ref, turned_ref, *refs):
    tiles, weights_ref = refs[:-1], refs[-1]
    place = Place(*sizes, tiles[0].shape[0])
    weights_ref[...] = bundle_weights(place, dz, tiles, bins_ref, lag_ref, turned_ref)


def corr_kernel(sizes, *refs):
    n_rows, n_cols = sizes
    lines, picked, part_ref = refs[:n_cols], refs[n_cols:-1], refs[-1]
    place = Place(n_rows, n_cols, lines[0].shape[0])
    for dz, picked_ref in enumerate(picked):
        corr_step(place, dz, lines, picked_ref, part_ref)


def end_kernel(sizes, dz, bins_ref, lag_ref, table_ref, turned_ref, *refs):
    n_rows, n_cols = sizes
    per_line = PAIR * n_rows
    count = (n_cols // PAIR) * per_line
    every, old_weights = refs[:count], refs[count : count + dz + 1]
    old_part_ref, corr_out, grad_out, weights_ref, staged_ref, picked_ref, part_ref = refs[count + dz + 1 : -3]
    corr_ref, grad_ref, sems = refs[-3:]
    copies = []

    def write(source, target):
        copy = pltpu.make_async_copy(source, target, sems.at[len(copies)])
        copy.start()
        copies.append(copy)

    tiles = every[dz * per_line :]
    lines = every[::n_rows]
    block, width = tiles[0].shape
    freqs = width // 2
    norm = 1.0 / np.sqrt(np.float32(width))
    place = Place(n_rows, n_cols, block)
    pick_step(place, dz, tiles, table_ref, staged_ref, picked_ref)
    corr_step(place, dz, lines, picked_ref, part_ref)
    here = place.inside(dz)
    wide = PAIR * block
    for lag in range(LAGS):
        cols = slice(lag * wide, (lag + 1) * wide)
        halves = []
        for half in range(part_ref.shape[0]):
            fresh = here & (place.half(dz) == half)
            halves.append(jnp.where(fresh, part_ref[half, :, cols], old_part_ref[half, :, cols]))
        corr_ref[lag] = jnp.concatenate(halves, axis=1) * norm
        write(corr_ref.at[lag], corr_out.at[lag])

    span = per_line * block
    fresh = bundle_weights(place, dz, tiles[-1:], bins_ref, lag_ref, turned_ref, per_line - 1)
    for at, old_ref in enumerate(old_weights[:-1]):
        weights_ref[:, at * span : (at + 1) * span] = old_ref[...]
    weights_ref[:, dz * span :] = jnp.concatenate([old_weights[-1][...], fresh], axis=1)

    for start in range(0, freqs, CHUNK):
        cols = slice(start, start + CHUNK)
        high = slice(freqs + start, freqs + start + CHUNK)
        reals = jnp.dot(weights_ref[...], stack(every, cols), preferred_element_type=jnp.float32)
        imags = jnp.dot(weights_ref[...], stack(every, high), preferred_element_type=jnp.float32)
        real_sum = jnp.zeros((block, CHUNK), jnp.float32)
        imag_sum = jnp.zeros((block, CHUNK), jnp.float32)
        for at, shift in enumerate(SHIFTS):
            real = reals[at * block : (at + 1) * block]
            imag = imags[at * block : (at + 1) * block]
            if shift == 0:
                real_sum, imag_sum = real_sum + real, imag_sum + imag
            else:
                cosine, sine = phase(table_ref, shift, cols)
                real_sum += real * cosine + imag * sine
                imag_sum += imag * cosine - real * sine
        grad_ref[:, cols] = real_sum * norm
        grad_ref[:, high] = imag_sum * norm
        write(grad_ref.at[:, cols], grad_out.at[:, cols])
        write(grad_ref.at[:, high], grad_out.at[:, high])
    for copy in copies:
        copy.wait()


def per_device(spectra, band_weights, lag_weights, selected_bins):
    n_rows = lax.axis_size("rows")
    n_cols = lax.axis_size("cols")
    n_lines = n_cols // PAIR
    n_bits = n_rows.bit_length() - 1
    block, width = spectra.shape
    freqs = width // 2
    vmem = pl.BlockSpec(memory_space=pltpu.VMEM)
    smem = pl.BlockSpec(memory_space=pltpu.SMEM)
    table = phase_table(freqs)

    def send(value, move):
        pairs = []
        for r in range(n_rows):
            for c in range(n_cols):
                to_row, to_line, to_core = move(r, c // PAIR, c % PAIR)
                pairs.append((r * n_cols + c, to_row * n_cols + to_line * PAIR + to_core))
        return lax.ppermute(value, ("rows", "cols"), pairs)

    def send_row(value, bit):
        return send(value, lambda r, z, k: (r ^ (1 << (bit if k == 0 else n_bits - 1 - bit)), z, k))

    def send_line(value, step):
        return send(value, lambda r, z, k: (r, z ^ step, k))

    def call(kernel, outs, operands, specs, out_space=vmem, **more):
        held = sum(x.size * x.dtype.itemsize for x in [*operands, *jax.tree.leaves(outs)])
        return pl.pallas_call(
            kernel,
            out_shape=outs,
            in_specs=specs,
            out_specs=jax.tree.map(lambda _: out_space, outs),
            compiler_params=pltpu.CompilerParams(vmem_limit_bytes=min(held + (12 << 20), 60 << 20)),
            **more,
        )(*operands)

    def shape(rows, dtype, *last):
        return jax.ShapeDtypeStruct((rows, *(last or (width,))), dtype)

    whitened = call(
        whiten_kernel,
        shape(block, jnp.bfloat16),
        (spectra, band_weights[None, :]),
        [pl.BlockSpec(memory_space=pltpu.HBM)] * 2,
        scratch_shapes=[
            pltpu.VMEM((block, width), spectra.dtype),
            pltpu.VMEM((1, freqs), jnp.float32),
            pltpu.SemaphoreType.DMA((2,)),
        ],
    )
    turned = call(
        rotate_kernel, shape(len(SHIFTS) * block, jnp.bfloat16), (table, whitened), [vmem] * 2
    )
    lines = [whitened]
    for dz in range(1, n_lines):
        low = dz & -dz
        lines.append(send_line(lines[dz ^ low], low))
    groups = []
    for dz in range(n_lines):
        group = [lines[dz]]
        for slot in range(1, n_rows):
            if dz % 2 and slot == n_rows - 1:
                group.append(send_line(groups[dz ^ 1][slot], 1))
            else:
                high = slot.bit_length() - 1
                group.append(send_row(group[slot ^ (1 << high)], high))
        groups.append(group)
    swapped = [[send(tile, lambda r, z, k: (r, z, k ^ 1)) for tile in group] for group in groups]
    n_row, n_col = n_cols * block, n_rows * block
    sizes = (n_rows, n_cols)
    every = [[*groups[dz], *swapped[dz]] for dz in range(n_lines)]
    weights_shape = shape(len(SHIFTS) * block, jnp.bfloat16, PAIR * n_rows * block)
    picked_shape = shape(LAGS * PAIR * block, jnp.bfloat16)
    staged = pltpu.VMEM((PAIR * block, width), jnp.bfloat16)
    part_shape = (n_rows // PAIR, n_row, LAGS * PAIR * block)
    common = [selected_bins, lag_weights, table, turned]
    weights, picked = [], []
    for dz in range(n_lines - 1):
        operands = [*common, *every[dz]]
        new_weights, new_picked = call(
            functools.partial(bundle_kernel, sizes, dz),
            (weights_shape, picked_shape),
            operands,
            [smem] * 2 + [vmem] * (len(operands) - 2),
            scratch_shapes=[staged],
        )
        weights.append(new_weights)
        picked.append(new_picked)
    last = n_lines - 1
    operands = [selected_bins, lag_weights, turned, *every[last][:-1]]
    weights.append(
        call(
            functools.partial(partial_kernel, sizes, last),
            shape(len(SHIFTS) * block, jnp.bfloat16, (PAIR * n_rows - 1) * block),
            operands,
            [smem] * 2 + [vmem] * (len(operands) - 2),
        )
    )
    lines = [tile for group in every for tile in group[::n_rows]]
    parts = call(
        functools.partial(corr_kernel, sizes),
        shape(part_shape[0], jnp.float32, *part_shape[1:]),
        [*lines, *picked],
        [vmem] * (n_cols + n_lines - 1),
    )
    operands = [*common, *(tile for group in every for tile in group), *weights, parts]
    correlations, gradient = call(
        functools.partial(end_kernel, sizes, n_lines - 1),
        (shape(LAGS, jnp.float32, n_row, n_col), shape(block, jnp.float32)),
        operands,
        [smem] * 2 + [vmem] * (len(operands) - 2),
        scratch_shapes=[
            pltpu.VMEM((len(SHIFTS) * block, n_rows * n_cols * block), jnp.bfloat16),
            staged,
            pltpu.VMEM(picked_shape.shape, picked_shape.dtype),
            pltpu.VMEM(part_shape, jnp.float32),
            pltpu.VMEM((LAGS, n_row, n_col), jnp.float32),
            pltpu.VMEM((block, width), jnp.float32),
            pltpu.SemaphoreType.DMA((LAGS + 2 * (freqs // CHUNK),)),
        ],
        out_space=pl.BlockSpec(memory_space=pltpu.HBM),
    )
    return correlations, gradient


def solution(mesh):
    placed = (P(("rows", "cols"), None), P(), P(), P())
    return jax.shard_map(
        per_device,
        mesh=mesh,
        in_specs=placed,
        out_specs=(P(None, "rows", "cols"), P(("rows", "cols"), None)),
        check_vma=False,
    )
```
